32 devices in a mesh: sx: 8 (over y, x, core), sy: 4 (over z).
Axes of the slice: x: 2, y: 2, z: 4, core: 2. Of those that a mesh axis runs over, the one named last changes fastest.
Arguments:
- adjoint_loads: float32 [8, 8, 2, 288, 128], P('sx', 'sy'), may hold values from -6 to 6
- dual_taut: bfloat16 [8, 8, 1152, 1152], P('sx', 'sy'), may hold values from -1 to 2
- dual_wrinkle: bfloat16 [8, 8, 1152, 1152], P('sx', 'sy'), may hold values from -1 to 2
- dirichlet_taut: bfloat16 [8, 8, 1152, 1152], P('sx', 'sy'), may hold values from -1 to 2
- dirichlet_wrinkle: bfloat16 [8, 8, 1152, 1152], P('sx', 'sy'), may hold values from -1 to 2
- coupling: bfloat16 [8, 8, 12, 1152], P('sx', 'sy'), may hold values from -0.25 to 0.25
- coarse_inverse: bfloat16 [256, 256], P('sx', 'sy'), may hold values from -1 to 2
- wrinkled: int32 [8, 8], P('sx', 'sy'), may hold values 0 or 1
- edge_lengths: int32 [8, 8, 2], P('sx', 'sy'), may hold values from 144 to 288
- corner_map: int32 [8, 8, 12], P('sx', 'sy'), may hold values from 0 to 255, as said below
Outputs:
- multipliers: float32 [8, 8, 2, 288, 128], P('sx', 'sy')
- preconditioned: float32 [8, 8, 2, 288, 128], P('sx', 'sy')
The draws below stay inside these ranges and needn't reach their ends.
Inputs may be any that keep to these rules, and one draw needn't show every extreme that they name: `corner_map`: each subdomain names 12 distinct coarse indices, three for each of its four grid corners; subdomains that meet at a grid corner name the same three indices for it; distinct grid corners name distinct indices.
All inputs are finite; a program needn't handle non-finite values. No bound on the sum of `wrinkled` on one device may be relied on, other than what follows from the above.
Results may differ from the reference program's by a relative error of at most 0.012.
Values may be sent and summed in bfloat16 or wider, within the bound.
A program may use at most 64 MiB of HBM per device.

```python
import jax
import jax.numpy as jnp
from jax import lax

ORDER = 1152
EDGE = 288
LOADS = 128
CORNERS = 12
ITERS = 2
SUB_ROWS = 8
SUB_COLS = 8
COARSE = 256


def dominant(key, lead, size, low, high, spread_off):
    diag_key, off_key = jax.random.split(key)
    diagonal = jax.random.uniform(diag_key, lead + (size,), jnp.float32, low, high)
    off_part = jnp.clip(jax.random.normal(off_key, lead + (size, size), jnp.float32), -4.0, 4.0)
    off_part = off_part * (spread_off / size ** 0.5)
    return (off_part + jnp.eye(size, dtype=jnp.float32) * diagonal[..., None]).astype(jnp.bfloat16)


def draw_dual_taut(key, part):
    return dominant(jax.random.fold_in(key, 11), (SUB_ROWS, SUB_COLS), ORDER, 0.5, 1.5, 0.5)


def draw_dual_wrinkle(key, part):
    return dominant(jax.random.fold_in(key, 12), (SUB_ROWS, SUB_COLS), ORDER, 0.3, 0.9, 0.3)


def draw_dirichlet_taut(key, part):
    return dominant(jax.random.fold_in(key, 13), (SUB_ROWS, SUB_COLS), ORDER, 0.5, 1.5, 0.5)


def draw_dirichlet_wrinkle(key, part):
    return dominant(jax.random.fold_in(key, 14), (SUB_ROWS, SUB_COLS), ORDER, 0.3, 0.9, 0.3)


def draw_coarse_inverse(key, part):
    return dominant(jax.random.fold_in(key, 15), (), COARSE, 0.5, 1.5, 0.8)


def draw_corner_map(key, part):
    shuffled = jax.random.permutation(jax.random.fold_in(key, 21), COARSE)
    row_ids = jnp.arange(SUB_ROWS)[:, None, None]
    column_ids = jnp.arange(SUB_COLS)[None, :, None]
    slot_ids = jnp.arange(CORNERS)[None, None, :]
    corner_slot = slot_ids // 3
    down_step = jnp.array([0, 0, 1, 1])[corner_slot]
    right_step = jnp.array([0, 1, 1, 0])[corner_slot]
    grid_point = (row_ids + down_step) * (SUB_COLS + 1) + column_ids + right_step
    return shuffled[3 * grid_point + slot_ids % 3].astype(jnp.int32)


def with_ends(drawn, own_key, smallest, largest):
    extent = drawn.shape
    place = [jax.random.randint(jax.random.fold_in(own_key, axis), (), 0, extent[axis]) for axis in range(len(extent))]
    drawn = drawn.at[tuple(place)].set(smallest)
    longest = extent.index(max(extent))
    place[longest] = (place[longest] + 1) % extent[longest]
    return drawn.at[tuple(place)].set(largest)


def steps_of(key, shape, pieces, smallest, high):
    def one(dim, blocks):
        heights = jax.random.uniform(jax.random.fold_in(jax.random.fold_in(key, 6), dim), (blocks,), jnp.float32, smallest / len(pieces), high / len(pieces))
        return jnp.repeat(jnp.exp(heights), shape[dim] // blocks).reshape((-1,) + (1,) * (len(shape) - dim - 1))

    level = one(*pieces[0])
    for cut in pieces[1:]:
        level = level * one(*cut)
    return level


def normal_values(own_key, shape, deviation, bound, cuts=(), held_as=jnp.bfloat16):
    values = jax.random.normal(own_key, shape, jnp.float32) * deviation
    if len(cuts) > 0:
        values = steps_of(own_key, shape, cuts, -0.22, 0.18) * values
    return jnp.clip(values, min=-bound, max=bound).astype(held_as)


def setup_inputs(seed: int = 0) -> dict:
    key_list = jax.random.split(jax.random.key(seed), 11)
    adjoint_loads = normal_values(key_list[0], (SUB_ROWS, SUB_COLS, 2, EDGE, LOADS), 1.0, 6.0, ((0, 8), (1, 4)), jnp.float32)
    dual_taut = draw_dual_taut(jax.random.fold_in(key_list[10], 71), 0)
    dual_wrinkle = draw_dual_wrinkle(jax.random.fold_in(key_list[10], 71), 0)
    dirichlet_taut = draw_dirichlet_taut(jax.random.fold_in(key_list[10], 71), 0)
    dirichlet_wrinkle = draw_dirichlet_wrinkle(jax.random.fold_in(key_list[10], 71), 0)
    coupling = normal_values(key_list[5], (SUB_ROWS, SUB_COLS, CORNERS, ORDER), (ORDER // 2) ** -0.5, 0.25, ((0, 8), (1, 4)))
    coarse_inverse = draw_coarse_inverse(jax.random.fold_in(key_list[10], 71), 0)
    wrinkled = with_ends((jax.random.randint(key_list[7], (SUB_ROWS, SUB_COLS), 0, 3) < 1).astype(jnp.int32), jax.random.fold_in(key_list[7], 1), 0, 1)
    edge_lengths = with_ends(jax.random.randint(key_list[8], (SUB_ROWS, SUB_COLS, 2), EDGE // 2, EDGE + 1), jax.random.fold_in(key_list[8], 1), EDGE // 2, EDGE).astype(jnp.int32)
    corner_map = draw_corner_map(jax.random.fold_in(key_list[10], 71), 0)
    return {"adjoint_loads": adjoint_loads, "dual_taut": dual_taut, "dual_wrinkle": dual_wrinkle, "dirichlet_taut": dirichlet_taut, "dirichlet_wrinkle": dirichlet_wrinkle, "coupling": coupling, "coarse_inverse": coarse_inverse, "wrinkled": wrinkled, "edge_lengths": edge_lengths, "corner_map": corner_map}


step_sizes = (0.55, 0.75)
momenta = (0.0, 0.15)


def edge_mask(edge_lengths):
    positions = jnp.arange(EDGE, dtype=jnp.int32)
    inside = positions[None, None, None, :] < edge_lengths[:, :, :, None]
    row_ids = jnp.arange(SUB_ROWS, dtype=jnp.int32)[:, None] + jnp.zeros((1, SUB_COLS), jnp.int32)
    column_ids = jnp.arange(SUB_COLS, dtype=jnp.int32)[None, :] + jnp.zeros((SUB_ROWS, 1), jnp.int32)
    exists = jnp.stack([column_ids < SUB_COLS - 1, row_ids < SUB_ROWS - 1], axis=2)
    return (inside & exists[:, :, :, None]).astype(jnp.float32)[..., None]


def spread(edges):
    east_edge = edges[:, :, 0]
    south_edge = edges[:, :, 1]
    west_edge = jnp.concatenate([jnp.zeros_like(east_edge[:, :1]), east_edge[:, :-1]], axis=1)
    north_edge = jnp.concatenate([jnp.zeros_like(south_edge[:1]), south_edge[:-1]], axis=0)
    return jnp.concatenate([east_edge, south_edge, -west_edge, -north_edge], axis=2)


def collect(local_part):
    west_part = local_part[:, :, 2 * EDGE:3 * EDGE]
    right_west = jnp.concatenate([west_part[:, 1:], jnp.zeros_like(west_part[:, :1])], axis=1)
    north_part = local_part[:, :, 3 * EDGE:]
    down_north = jnp.concatenate([north_part[1:], jnp.zeros_like(north_part[:1])], axis=0)
    return jnp.stack([local_part[:, :, :EDGE] - right_west, local_part[:, :, EDGE:2 * EDGE] - down_north], axis=2)


def paired(taut, wrinkle, wrinkled, vectors):
    def one_row(operands):
        taut_row, wrinkle_row, flag_row, vector_row = operands
        vector_wide = vector_row.astype(jnp.float32)
        base_part = jnp.einsum("sij,sjl->sil", taut_row.astype(jnp.float32), vector_wide)
        extra_part = jnp.einsum("sij,sjl->sil", wrinkle_row.astype(jnp.float32), vector_wide)
        return base_part + flag_row.astype(jnp.float32)[:, None, None] * extra_part

    return lax.map(one_row, (taut, wrinkle, wrinkled, vectors))


def coarse_term(coupling, corner_map, coarse_inverse, vectors):
    coupling_wide = coupling.astype(jnp.float32)
    corner_terms = jnp.einsum("rskj,rsjl->rskl", coupling_wide, vectors.astype(jnp.float32))
    corner_index = corner_map.reshape(-1).astype(jnp.int32)
    gathered = jnp.zeros((COARSE, LOADS), jnp.float32).at[corner_index].add(corner_terms.reshape(-1, LOADS))
    solved = jnp.dot(coarse_inverse, gathered.astype(jnp.bfloat16), preferred_element_type=jnp.float32).astype(jnp.bfloat16)
    selected = solved[corner_index].reshape(SUB_ROWS, SUB_COLS, CORNERS, LOADS)
    return jnp.einsum("rskj,rskl->rsjl", coupling_wide, selected.astype(jnp.float32))


def reference(adjoint_loads, dual_taut, dual_wrinkle, dirichlet_taut, dirichlet_wrinkle, coupling, coarse_inverse, wrinkled, edge_lengths, corner_map):
    masking = edge_mask(edge_lengths)
    loads = adjoint_loads * masking

    def dual_apply(incoming):
        vectors = spread(incoming.astype(jnp.bfloat16))
        local_part = paired(dual_taut, dual_wrinkle, wrinkled, vectors)
        local_part = local_part + coarse_term(coupling, corner_map, coarse_inverse, vectors)
        return collect(local_part) * masking

    def precondition(incoming):
        vectors = spread((0.5 * incoming).astype(jnp.bfloat16))
        return 0.5 * collect(paired(dirichlet_taut, dirichlet_wrinkle, wrinkled, vectors)) * masking

    multipliers = jnp.zeros_like(loads)
    direction = jnp.zeros_like(loads)
    residual = loads
    for number in range(ITERS):
        direction = precondition(residual) + momenta[number] * direction
        multipliers = multipliers + step_sizes[number] * direction
        residual = loads - dual_apply(multipliers)
    return multipliers, precondition(residual)
```

```python
import functools

import jax
import jax.numpy as jnp
from jax import lax
from jax.experimental import pallas as pl
from jax.experimental.pallas import tpu as pltpu
from jax.sharding import PartitionSpec as P

ITERS = 2
step_sizes = (0.55, 0.75)
momenta = (0.0, 0.15)

MESH = pl.DeviceIdType.MESH
SLOT = 16
F32 = jnp.float32
BF16 = jnp.bfloat16


def kernel(
    nr, ns,
    loads_ref, dual_t, dual_w, diri_t, diri_w, coup_ref, cinv_ref, wr_ref, len_ref, cm_ref,
    mult_out, prec_out,
    am, aw, bm, bw, vec, loc, snd, rcv, ld, mu, di, cpad, meta, mz, mx, cf, kmat, ts, tp, ys, yr,
    mat_sem, h_send, h_recv, mz_send, mz_recv, mx_send, mx_recv, cz_send, cz_recv, cx_send, cx_recv,
    t_send, t_recv, y_send, y_recv,
):
    r, s = lax.axis_index("sx"), lax.axis_index("sy")
    per = loads_ref.shape[1]
    edge, width = loads_ref.shape[3], loads_ref.shape[4]
    corners = coup_ref.shape[2]
    tr, tc = cinv_ref.shape
    order = nr * tr
    rows = per * SLOT
    has_left, has_right = s > 0, s < ns - 1
    has_up, has_down = r > 0, r < nr - 1
    FROM_LEFT, FROM_RIGHT, FROM_UP, FROM_DOWN = 0, 1, 2, 2 + per

    loads_in = []
    for i, (src, dst) in enumerate(((diri_t, am), (diri_w, aw), (dual_t, bm), (dual_w, bw))):
        for c in range(per):
            loads_in.append(pltpu.make_async_copy(src.at[0, c], dst.at[c], mat_sem.at[i * per + c]))
    for c in range(per):
        for i in (0, 1):
            loads_in[i * per + c].start()
    for c in range(per):
        for i in (2, 3):
            loads_in[i * per + c].start()

    barrier = pltpu.get_barrier_semaphore()
    for k in range(1, nr):
        pl.semaphore_signal(barrier, inc=1, device_id={"sx": lax.rem(r + k, nr)}, device_id_type=MESH)
    for k in range(1, ns):
        pl.semaphore_signal(barrier, inc=1, device_id={"sy": lax.rem(s + k, ns)}, device_id_type=MESH)

    meta[...] = jnp.full(meta.shape, -1, jnp.int32)
    for c in range(per):
        for m in range(corners):
            meta[c * SLOT + m : c * SLOT + m + 1, :] = jnp.full((1, 128), cm_ref[0, c, m], jnp.int32)
        east = len_ref[0, c, 0]
        if c == per - 1:
            east = jnp.where(has_right, east, 0)
        south = jnp.where(has_down, len_ref[0, c, 1], 0)
        meta[rows + c : rows + c + 1, :] = jnp.full((1, 128), east, jnp.int32)
        meta[rows + per + c : rows + per + c + 1, :] = jnp.full((1, 128), south, jnp.int32)
    mz[pl.ds(s, 1)] = meta[...][None]
    mx[pl.ds(r, 1)] = meta[...][None]
    cf[pl.ds(s, 1), pl.ds(pl.multiple_of(r * tr, 8), tr), :] = cinv_ref[...].astype(F32)[None]

    positions = lax.broadcasted_iota(jnp.int32, (edge, width), 0)

    def live(length_row):
        return positions < jnp.broadcast_to(length_row, (edge, width))

    own_mask = {}
    for c in range(per):
        own_mask[c] = meta[rows + c : rows + c + 1, :]
        own_mask[per + c] = meta[rows + per + c : rows + per + c + 1, :]

    EAST, SOUTH, NORTH, WEST = 0, per, 2 * per, 3 * per

    def halo(k, slot, where_to):
        axis, shift = where_to
        index = (r if axis == "sx" else s) + shift
        return pltpu.make_async_remote_copy(
            src_ref=snd.at[k, slot], dst_ref=rcv.at[k, slot],
            send_sem=h_send.at[k, slot], recv_sem=h_recv.at[k, slot],
            device_id={axis: index}, device_id_type=MESH,
        )

    def route(slot):
        if slot == FROM_LEFT:
            return ("sy", 1), has_right, has_left
        if slot == FROM_RIGHT:
            return ("sy", -1), has_left, has_right
        if slot < FROM_DOWN:
            return ("sx", 1), has_down, has_up
        return ("sx", -1), has_up, has_down

    def send(k, slot, value):
        snd[k, slot] = value.astype(BF16)
        to, can, _ = route(slot)

        @pl.when(can)
        def _():
            halo(k, slot, to).start()

    def arrive(k, slot):
        to, _, gets = route(slot)

        @pl.when(gets)
        def _():
            halo(k, slot, to).wait_recv()

    def left_behind(k, slot):
        to, can, _ = route(slot)

        @pl.when(can)
        def _():
            halo(k, slot, to).wait_send()

    def put(kind, c, value):
        value = value.astype(BF16)
        if kind == EAST:
            vec[c, 0:edge] = value
            if c + 1 < per:
                vec[c + 1, 2 * edge : 3 * edge] = -value
        elif kind == SOUTH:
            vec[c, edge : 2 * edge] = value
        elif kind == NORTH:
            vec[c, 3 * edge :] = -value
        else:
            vec[0, 2 * edge : 3 * edge] = -value

    for c in range(per):
        for kind in (0, 1):
            e = kind * per + c
            value = jnp.where(live(own_mask[e]), loads_ref[0, c, kind], 0.0)
            ld[e] = value
            put(EAST if kind == 0 else SOUTH, c, 0.5 * value)
            if kind == 1:
                snd[0, FROM_UP + c] = value.astype(BF16)
            elif c == per - 1:
                snd[0, FROM_LEFT] = value.astype(BF16)
    pl.semaphore_wait(barrier, nr - 1 + ns - 1)
    for slot in [FROM_LEFT] + [FROM_UP + c for c in range(per)]:
        to, can, _ = route(slot)

        @pl.when(can)
        def _(to=to, slot=slot):
            halo(0, slot, to).start()

    def peer_copy(axis, k, src, dst, ssem, rsem):
        n, me = (nr, r) if axis == "sx" else (ns, s)
        return pltpu.make_async_remote_copy(
            src_ref=src, dst_ref=dst, send_sem=ssem.at[k], recv_sem=rsem.at[k],
            device_id={axis: lax.rem(me + k, n)}, device_id_type=MESH,
        )

    my_rows = pl.ds(pl.multiple_of(r * tr, 8), tr)
    cz = [peer_copy("sy", k, cf.at[s, my_rows], cf.at[s, my_rows], cz_send, cz_recv) for k in range(1, ns)]
    mzc = [peer_copy("sy", k, meta, mz.at[s], mz_send, mz_recv) for k in range(1, ns)]
    mxc = [peer_copy("sx", k, meta, mx.at[r], mx_send, mx_recv) for k in range(1, nr)]
    cx = [peer_copy("sx", k, cf.at[:, my_rows], cf.at[:, my_rows], cx_send, cx_recv) for k in range(1, nr)]
    for copy in cz + mzc + mxc:
        copy.start()

    cpad[...] = jnp.zeros(cpad.shape, BF16)
    for c in range(per):
        cpad[c, 0:corners] = coup_ref[0, c]

    def combine(c, main, extra):
        flag = jnp.full((1, 1), wr_ref[0, c], jnp.int32).astype(F32).astype(BF16)
        size = main.shape[1]
        step = 128

        def body(i, _):
            part = pl.ds(pl.multiple_of(i * step, step), step)
            main[c, part] = main[c, part] + flag * extra[c, part]
            return 0

        lax.fori_loop(0, size // step, body, 0)

    def product(mat, c, e):
        return jnp.dot(mat[c, e * edge : (e + 1) * edge, :], vec[c], preferred_element_type=F32)

    blocks = [(c, 3) for c in range(per)] + [(c, 1) for c in range(per)]
    blocks += [(per - 1, 0), (0, 2)]
    blocks += [(c, 0) for c in range(per - 1)] + [(c, 2) for c in range(1, per)]

    def slot_of(c, e):
        if e == 3:
            return FROM_DOWN + c
        if e == 1:
            return FROM_UP + c
        if e == 0 and c == per - 1:
            return FROM_LEFT
        if e == 2 and c == 0:
            return FROM_RIGHT
        return None

    def deliver(k, c, e, value, last):
        loc[c, e * edge : (e + 1) * edge] = value
        slot = slot_of(c, e)
        if slot is not None and not (last and e in (0, 1)):
            send(k, slot, value)

    def local_rows(c, e):
        return loc[c, e * edge : (e + 1) * edge]

    def mask_of(kind, c):
        if kind == EAST:
            return live(own_mask[c])
        if kind == SOUTH:
            return live(own_mask[per + c])
        if kind == NORTH:
            row = mx[jnp.maximum(r - 1, 0), rows + per + c : rows + per + c + 1, :]
            return live(jnp.where(has_up, row, 0))
        row = mz[jnp.maximum(s - 1, 0), rows + per - 1 : rows + per, :]
        return live(jnp.where(has_left, row, 0))

    def gathered(k, kind, c):
        if kind == EAST:
            if c + 1 < per:
                return local_rows(c, 0) - local_rows(c + 1, 2)
            arrive(k, FROM_RIGHT)
            return local_rows(c, 0) - rcv[k, FROM_RIGHT].astype(F32)
        if kind == SOUTH:
            arrive(k, FROM_DOWN + c)
            return local_rows(c, 1) - rcv[k, FROM_DOWN + c].astype(F32)
        if kind == NORTH:
            arrive(k, FROM_UP + c)
            return rcv[k, FROM_UP + c].astype(F32) - local_rows(c, 3)
        arrive(k, FROM_LEFT)
        return rcv[k, FROM_LEFT].astype(F32) - local_rows(0, 2)

    inner = [(EAST, c) for c in range(per)]
    everything = inner + [(WEST, 0)] + [(SOUTH, c) for c in range(per)] + [(NORTH, c) for c in range(per)]

    for c in range(per):
        loads_in[c].wait()
        loads_in[per + c].wait()
        combine(c, am, aw)
    for slot, kind, c, there in [(FROM_LEFT, WEST, 0, has_left)] + [(FROM_UP + c, NORTH, c, has_up) for c in range(per)]:
        arrive(0, slot)
        value = jnp.where(jnp.broadcast_to(there, (edge, width)), rcv[0, slot].astype(F32), 0.0)
        ld[kind + c] = value
        put(kind, c, 0.5 * value)

    def setup_middle():
        for k in range(ns - 1):
            cz[k].wait_recv()
            mzc[k].wait_recv()
        for copy in cx:
            copy.start()
        for k in range(nr - 1):
            mxc[k].wait_recv()

    def setup_end():
        for k in range(nr - 1):
            cx[k].wait_recv()
        row_index = mz[:, 0:rows, :].reshape(ns * rows, 128)[:, 0:1]
        plane_index = mx[:, 0:rows, :].reshape(nr * rows, 128)[:, 0:1]
        row_pick = (
            jnp.broadcast_to(row_index, (ns * rows, order))
            == lax.broadcasted_iota(jnp.int32, (ns * rows, order), 1)
        ).astype(F32).astype(BF16)
        total = jnp.zeros((ns * rows, nr * rows), F32)
        for q in range(ns):
            picked = jnp.dot(row_pick, cf[q].astype(BF16), preferred_element_type=F32).astype(BF16)
            plane_pick = (
                jnp.broadcast_to(plane_index, (nr * rows, tc))
                == lax.broadcasted_iota(jnp.int32, (nr * rows, tc), 1) + q * tc
            ).astype(F32).astype(BF16)
            total = total + lax.dot_general(
                picked, plane_pick, (((1,), (1,)), ((), ())), preferred_element_type=F32
            )
        kmat[...] = total.astype(BF16)

    halo_round = 1
    for number in range(ITERS):
        for c, e in blocks:
            deliver(halo_round, c, e, product(am, c, e), False)
        if number == 0:
            setup_middle()
            for c in range(per):
                loads_in[2 * per + c].wait()
                loads_in[3 * per + c].wait()
                combine(c, bm, bw)
            setup_end()
        for kind, c in everything:
            value = jnp.where(mask_of(kind, c), 0.5 * gathered(halo_round, kind, c), 0.0)
            if number == 0:
                iterate = step_sizes[0] * value
            else:
                value = value + momenta[number] * di[kind + c]
                iterate = mu[kind + c] + step_sizes[number] * value
            if number < ITERS - 1:
                di[kind + c] = value
                mu[kind + c] = iterate
            elif kind in (EAST, SOUTH):
                mult_out[0, c, 0 if kind == EAST else 1] = iterate
            put(kind, c, iterate)
        halo_round += 1

        for c in range(per):
            terms = jnp.dot(cpad[c], vec[c], preferred_element_type=F32).astype(BF16)
            ts[number, c * SLOT : (c + 1) * SLOT] = terms
            tp[number, pl.ds(r, 1), c * SLOT : (c + 1) * SLOT] = terms[None]
        tcopies = [
            peer_copy("sx", k, ts.at[number], tp.at[number, r], t_send.at[number], t_recv.at[number])
            for k in range(1, nr)
        ]
        for copy in tcopies:
            copy.start()
        half = len(blocks) // 2
        for c, e in blocks[:half]:
            loc[c, e * edge : (e + 1) * edge] = product(bm, c, e)
        for copy in tcopies:
            copy.wait_recv()
        partial = jnp.dot(kmat[...], tp[number].reshape(nr * rows, 128), preferred_element_type=F32)
        ys[number] = partial.astype(BF16).reshape(ns, rows, 128)
        yr[number, pl.ds(s, 1)] = ys[number, pl.ds(s, 1)]
        ycopies = [
            peer_copy(
                "sy", k, ys.at[number, lax.rem(s + k, ns)], yr.at[number, s],
                y_send.at[number], y_recv.at[number],
            )
            for k in range(1, ns)
        ]
        for copy in ycopies:
            copy.start()
        for c, e in blocks[half:]:
            loc[c, e * edge : (e + 1) * edge] = product(bm, c, e)
        for copy in ycopies:
            copy.wait_recv()
        solved = yr[number, 0].astype(F32)
        for q in range(1, ns):
            solved = solved + yr[number, q].astype(F32)
        solved = solved.astype(BF16)
        for c, e in blocks:
            coarse = lax.dot_general(
                cpad[c, :, e * edge : (e + 1) * edge] if (e * edge) % 128 == 0 and edge % 128 == 0 else cpad[c][:, e * edge : (e + 1) * edge],
                solved[c * SLOT : (c + 1) * SLOT], (((0,), (0,)), ((), ())), preferred_element_type=F32,
            )
            deliver(halo_round, c, e, local_rows(c, e) + coarse, False)
        for kind, c in everything:
            value = jnp.where(mask_of(kind, c), gathered(halo_round, kind, c), 0.0)
            put(kind, c, 0.5 * (ld[kind + c] - value))
        halo_round += 1
        for copy in tcopies + ycopies:
            copy.wait_send()

    for c, e in blocks:
        deliver(halo_round, c, e, product(am, c, e), True)
    for c in range(per):
        for kind in (EAST, SOUTH):
            value = jnp.where(mask_of(kind, c), 0.5 * gathered(halo_round, kind, c), 0.0)
            prec_out[0, c, 0 if kind == EAST else 1] = value

    for copy in cz + mzc + mxc + cx:
        copy.wait_send()
    down_right = [FROM_LEFT] + [FROM_UP + c for c in range(per)]
    up_left = [FROM_RIGHT] + [FROM_DOWN + c for c in range(per)]
    for k in range(halo_round + 1):
        slots = down_right if k == 0 else up_left if k == halo_round else down_right + up_left
        for slot in slots:
            left_behind(k, slot)


def local(nr, ns, *args):
    adjoint_loads, dual_taut, coupling, coarse_inverse = args[0], args[1], args[5], args[6]
    per, edge, width = adjoint_loads.shape[1], adjoint_loads.shape[3], adjoint_loads.shape[4]
    size = dual_taut.shape[-1]
    tr, tc = coarse_inverse.shape
    rows = per * SLOT
    rounds = 2 * ITERS + 2
    slots = 2 + 2 * per
    meta_rows = rows + -(-2 * per // 8) * 8
    dma = pltpu.SemaphoreType.DMA
    vmem = pl.BlockSpec(memory_space=pltpu.VMEM)
    smem = pl.BlockSpec(memory_space=pltpu.SMEM)
    hbm = pl.BlockSpec(memory_space=pl.ANY)
    mats = [pltpu.VMEM((per, size, size), BF16)] * 4
    scratch = mats + [
        pltpu.VMEM((per, size, width), BF16),
        pltpu.VMEM((per, size, width), F32),
        pltpu.VMEM((rounds, slots, edge, width), BF16),
        pltpu.VMEM((rounds, slots, edge, width), BF16),
        pltpu.VMEM((3 * per + 1, edge, width), F32),
        pltpu.VMEM((3 * per + 1, edge, width), F32),
        pltpu.VMEM((3 * per + 1, edge, width), F32),
        pltpu.VMEM((per, SLOT, size), BF16),
        pltpu.VMEM((meta_rows, 128), jnp.int32),
        pltpu.VMEM((ns, meta_rows, 128), jnp.int32),
        pltpu.VMEM((nr, meta_rows, 128), jnp.int32),
        pltpu.VMEM((ns, nr * tr, tc), F32),
        pltpu.VMEM((ns * rows, nr * rows), BF16),
        pltpu.VMEM((ITERS, rows, width), BF16),
        pltpu.VMEM((ITERS, nr, rows, width), BF16),
        pltpu.VMEM((ITERS, ns, rows, width), BF16),
        pltpu.VMEM((ITERS, ns, rows, width), BF16),
        dma((4 * per,)),
        dma((rounds, slots)), dma((rounds, slots)),
        dma((ns,)), dma((ns,)),
        dma((nr,)), dma((nr,)),
        dma((ns,)), dma((ns,)),
        dma((nr,)), dma((nr,)),
        dma((ITERS, nr)), dma((ITERS, nr)),
        dma((ITERS, ns)), dma((ITERS, ns)),
    ]
    out = jax.ShapeDtypeStruct(adjoint_loads.shape, F32)
    return pl.pallas_call(
        functools.partial(kernel, nr, ns),
        out_shape=(out, out),
        in_specs=[vmem, hbm, hbm, hbm, hbm, vmem, vmem, smem, smem, smem],
        out_specs=(vmem, vmem),
        scratch_shapes=scratch,
        compiler_params=pltpu.CompilerParams(
            collective_id=0, has_side_effects=True, vmem_limit_bytes=60 * 1024 * 1024
        ),
    )(*args)


def solution(mesh):
    placed = (
        P("sx", "sy", None, None, None),
        P("sx", "sy", None, None),
        P("sx", "sy", None, None),
        P("sx", "sy", None, None),
        P("sx", "sy", None, None),
        P("sx", "sy", None, None),
        P("sx", "sy"),
        P("sx", "sy"),
        P("sx", "sy", None),
        P("sx", "sy", None),
    )
    return jax.shard_map(
        functools.partial(local, mesh.shape["sx"], mesh.shape["sy"]),
        mesh=mesh,
        in_specs=placed,
        out_specs=(P("sx", "sy", None, None, None), P("sx", "sy", None, None, None)),
        check_vma=False,
    )
```

```python
import functools

import jax
import jax.numpy as jnp
from jax import lax
from jax.experimental import pallas as pl
from jax.experimental.pallas import tpu as pltpu
from jax.sharding import PartitionSpec as P

ITERS = 2
step_sizes = (0.55, 0.75)
momenta = (0.0, 0.15)

MESH = pl.DeviceIdType.MESH
SLOT = 16
F32 = jnp.float32
BF16 = jnp.bfloat16


def kernel(
    nr, ns,
    loads_ref, dual_t, dual_w, diri_t, diri_w, coup_ref, cinv_ref, wr_ref, len_ref, cm_ref,
    mult_out, prec_out,
    am, aw, bm, bw, vec, loc, snd, rcv, ld, mu, di, cpad, ncp, ct, nct, meta, mz, mx, cf, kmat, ts, tp, ys, yr, yo, yn,
    mat_sem, h_send, h_recv, mz_send, mz_recv, mx_send, mx_recv, cz_send, cz_recv, cx_send, cx_recv,
    t_send, t_recv, y_send, y_recv, c_send, c_recv, n_send, n_recv,
):
    r, s = lax.axis_index("sx"), lax.axis_index("sy")
    per = loads_ref.shape[1]
    edge, width = loads_ref.shape[3], loads_ref.shape[4]
    corners = coup_ref.shape[1]
    tr, tc = cinv_ref.shape
    order = nr * tr
    rows = per * SLOT
    has_left, has_right = s > 0, s < ns - 1
    has_up, has_down = r > 0, r < nr - 1
    FROM_LEFT, FROM_RIGHT, FROM_UP, FROM_DOWN = 0, 1, 2, 2 + per

    loads_in = []
    for i, (src, dst) in enumerate(((diri_t, am), (diri_w, aw), (dual_t, bm), (dual_w, bw))):
        for c in range(per):
            loads_in.append(pltpu.make_async_copy(src.at[0, c], dst.at[c], mat_sem.at[i * per + c]))
    for c in range(per):
        for i in (0, 1):
            loads_in[i * per + c].start()
    barrier = pltpu.get_barrier_semaphore()
    for k in range(1, nr):
        pl.semaphore_signal(barrier, inc=1, device_id={"sx": lax.rem(r + k, nr)}, device_id_type=MESH)
    for k in range(1, ns):
        pl.semaphore_signal(barrier, inc=1, device_id={"sy": lax.rem(s + k, ns)}, device_id_type=MESH)

    meta[...] = jnp.full(meta.shape, -1, jnp.int32)
    for c in range(per):
        for m in range(corners):
            meta[c * SLOT + m : c * SLOT + m + 1, :] = jnp.full((1, 128), cm_ref[0, c, m], jnp.int32)
        east = len_ref[0, c, 0]
        if c == per - 1:
            east = jnp.where(has_right, east, 0)
        south = jnp.where(has_down, len_ref[0, c, 1], 0)
        meta[rows + c : rows + c + 1, :] = jnp.full((1, 128), east, jnp.int32)
        meta[rows + per + c : rows + per + c + 1, :] = jnp.full((1, 128), south, jnp.int32)
    mz[pl.ds(s, 1)] = meta[...][None]
    mx[pl.ds(r, 1)] = meta[...][None]
    cf[pl.ds(s, 1), pl.ds(pl.multiple_of(r * tr, 8), tr), :] = cinv_ref[...].astype(F32)[None]

    positions = lax.broadcasted_iota(jnp.int32, (edge, width), 0)

    def live(length_row):
        return positions < jnp.broadcast_to(length_row, (edge, width))

    own_mask = {}
    for c in range(per):
        own_mask[c] = meta[rows + c : rows + c + 1, :]
        own_mask[per + c] = meta[rows + per + c : rows + per + c + 1, :]

    EAST, SOUTH, NORTH, WEST = 0, per, 2 * per, 3 * per

    def source_of(slot):
        if slot == FROM_LEFT:
            return per - 1
        if slot == FROM_RIGHT:
            return 0
        return slot - (FROM_UP if slot < FROM_DOWN else FROM_DOWN)

    def neighbour(src, dst, ssem, rsem, where_to):
        axis, shift = where_to
        index = (r if axis == "sx" else s) + shift
        return pltpu.make_async_remote_copy(
            src_ref=src, dst_ref=dst, send_sem=ssem, recv_sem=rsem,
            device_id={axis: index}, device_id_type=MESH,
        )

    def halo(k, slot, where_to):
        return neighbour(
            snd.at[k, slot], rcv.at[k, slot], h_send.at[k, slot], h_recv.at[k, slot], where_to
        )

    def coupling_copy(slot, where_to):
        return neighbour(cpad.at[source_of(slot)], ncp.at[slot], c_send.at[slot], c_recv.at[slot], where_to)

    def solved_copy(k, slot, where_to):
        return neighbour(
            yo.at[k, source_of(slot)], yn.at[k, slot], n_send.at[k, slot], n_recv.at[k, slot], where_to
        )

    def route(slot):
        if slot == FROM_LEFT:
            return ("sy", 1), has_right, has_left
        if slot == FROM_RIGHT:
            return ("sy", -1), has_left, has_right
        if slot < FROM_DOWN:
            return ("sx", 1), has_down, has_up
        return ("sx", -1), has_up, has_down

    all_slots = range(2 + 2 * per)

    def if_sending(slot, act):
        to, can, _ = route(slot)

        @pl.when(can)
        def _():
            act(to)

    def if_getting(slot, act):
        to, _, gets = route(slot)

        @pl.when(gets)
        def _():
            act(to)

    def send(k, slot, value):
        snd[k, slot] = value.astype(BF16)
        to, can, _ = route(slot)

        @pl.when(can)
        def _():
            halo(k, slot, to).start()

    def arrive(k, slot):
        to, _, gets = route(slot)

        @pl.when(gets)
        def _():
            halo(k, slot, to).wait_recv()

    def left_behind(k, slot):
        to, can, _ = route(slot)

        @pl.when(can)
        def _():
            halo(k, slot, to).wait_send()

    def put(kind, c, value):
        value = value.astype(BF16)
        if kind == EAST:
            vec[c, 0:edge] = value
            if c + 1 < per:
                vec[c + 1, 2 * edge : 3 * edge] = -value
        elif kind == SOUTH:
            vec[c, edge : 2 * edge] = value
        elif kind == NORTH:
            vec[c, 3 * edge :] = -value
        else:
            vec[0, 2 * edge : 3 * edge] = -value

    for c in range(per):
        for kind in (0, 1):
            e = kind * per + c
            value = jnp.where(live(own_mask[e]), loads_ref[0, c, kind], 0.0)
            ld[e] = value
            put(EAST if kind == 0 else SOUTH, c, 0.5 * value)
            if kind == 1:
                snd[0, FROM_UP + c] = value.astype(BF16)
            elif c == per - 1:
                snd[0, FROM_LEFT] = value.astype(BF16)
    pl.semaphore_wait(barrier, nr - 1 + ns - 1)
    for slot in [FROM_LEFT] + [FROM_UP + c for c in range(per)]:
        to, can, _ = route(slot)

        @pl.when(can)
        def _(to=to, slot=slot):
            halo(0, slot, to).start()

    def peer_copy(axis, k, src, dst, ssem, rsem):
        n, me = (nr, r) if axis == "sx" else (ns, s)
        return pltpu.make_async_remote_copy(
            src_ref=src, dst_ref=dst, send_sem=ssem.at[k], recv_sem=rsem.at[k],
            device_id={axis: lax.rem(me + k, n)}, device_id_type=MESH,
        )

    my_rows = pl.ds(pl.multiple_of(r * tr, 8), tr)
    cz = [peer_copy("sy", k, cf.at[s, my_rows], cf.at[s, my_rows], cz_send, cz_recv) for k in range(1, ns)]
    mzc = [peer_copy("sy", k, meta, mz.at[s], mz_send, mz_recv) for k in range(1, ns)]
    mxc = [peer_copy("sx", k, meta, mx.at[r], mx_send, mx_recv) for k in range(1, nr)]
    cx = [peer_copy("sx", k, cf.at[:, my_rows], cf.at[:, my_rows], cx_send, cx_recv) for k in range(1, nr)]
    for copy in cz + mzc + mxc:
        copy.start()

    cpad[...] = jnp.zeros(cpad.shape, BF16)
    for c in range(per):
        cpad[c, 0:corners] = coup_ref[0, :, c, :]

    for slot in all_slots:
        if_sending(slot, lambda to, slot=slot: coupling_copy(slot, to).start())

    def combine(c, main, extra):
        flag = jnp.full((1, 1), wr_ref[0, c], jnp.int32).astype(F32).astype(BF16)
        size = main.shape[1]
        step = 128

        def body(i, _):
            part = pl.ds(pl.multiple_of(i * step, step), step)
            main[c, part] = main[c, part] + flag * extra[c, part]
            return 0

        lax.fori_loop(0, size // step, body, 0)

    def product(mat, c, e):
        return jnp.dot(mat[c, e * edge : (e + 1) * edge, :], vec[c], preferred_element_type=F32)

    blocks = [(c, 3) for c in range(per)] + [(c, 1) for c in range(per)]
    blocks += [(per - 1, 0), (0, 2)]
    blocks += [(c, 0) for c in range(per - 1)] + [(c, 2) for c in range(1, per)]

    def slot_of(c, e):
        if e == 3:
            return FROM_DOWN + c
        if e == 1:
            return FROM_UP + c
        if e == 0 and c == per - 1:
            return FROM_LEFT
        if e == 2 and c == 0:
            return FROM_RIGHT
        return None

    def deliver(k, c, e, value, last):
        loc[c, e * edge : (e + 1) * edge] = value
        slot = slot_of(c, e)
        if slot is not None and not (last and e in (0, 1)):
            send(k, slot, value)

    def local_rows(c, e):
        return loc[c, e * edge : (e + 1) * edge]

    def mask_of(kind, c):
        if kind == EAST:
            return live(own_mask[c])
        if kind == SOUTH:
            return live(own_mask[per + c])
        if kind == NORTH:
            row = mx[jnp.maximum(r - 1, 0), rows + per + c : rows + per + c + 1, :]
            return live(jnp.where(has_up, row, 0))
        row = mz[jnp.maximum(s - 1, 0), rows + per - 1 : rows + per, :]
        return live(jnp.where(has_left, row, 0))

    def gathered(k, kind, c):
        if kind == EAST:
            if c + 1 < per:
                return local_rows(c, 0) - local_rows(c + 1, 2)
            arrive(k, FROM_RIGHT)
            return local_rows(c, 0) - rcv[k, FROM_RIGHT].astype(F32)
        if kind == SOUTH:
            arrive(k, FROM_DOWN + c)
            return local_rows(c, 1) - rcv[k, FROM_DOWN + c].astype(F32)
        if kind == NORTH:
            arrive(k, FROM_UP + c)
            return rcv[k, FROM_UP + c].astype(F32) - local_rows(c, 3)
        arrive(k, FROM_LEFT)
        return rcv[k, FROM_LEFT].astype(F32) - local_rows(0, 2)

    inner = [(EAST, c) for c in range(per)]
    everything = inner + [(WEST, 0)] + [(SOUTH, c) for c in range(per)] + [(NORTH, c) for c in range(per)]

    for c in range(per):
        loads_in[c].wait()
        loads_in[per + c].wait()
        loads_in[2 * per + c].start()
        loads_in[3 * per + c].start()
        combine(c, am, aw)
    for slot, kind, c, there in [(FROM_LEFT, WEST, 0, has_left)] + [(FROM_UP + c, NORTH, c, has_up) for c in range(per)]:
        arrive(0, slot)
        value = jnp.where(jnp.broadcast_to(there, (edge, width)), rcv[0, slot].astype(F32), 0.0)
        ld[kind + c] = value
        put(kind, c, 0.5 * value)

    def setup_middle():
        for k in range(ns - 1):
            cz[k].wait_recv()
            mzc[k].wait_recv()
        for copy in cx:
            copy.start()
        for k in range(nr - 1):
            mxc[k].wait_recv()

    def setup_end():
        for c in range(per):
            ct[c] = cpad[c].astype(F32).T.astype(BF16)
        for slot in all_slots:
            if_getting(slot, lambda to, slot=slot: coupling_copy(slot, to).wait_recv())
            e = 0 if slot == FROM_LEFT else 2 if slot == FROM_RIGHT else 1 if slot < FROM_DOWN else 3
            nct[slot] = ncp[slot].astype(F32).T[e * edge : (e + 1) * edge].astype(BF16)
        for k in range(nr - 1):
            cx[k].wait_recv()
        row_index = mz[:, 0:rows, :].reshape(ns * rows, 128)[:, 0:1]
        plane_index = mx[:, 0:rows, :].reshape(nr * rows, 128)[:, 0:1]
        row_pick = (
            jnp.broadcast_to(row_index, (ns * rows, order))
            == lax.broadcasted_iota(jnp.int32, (ns * rows, order), 1)
        ).astype(F32).astype(BF16)
        total = jnp.zeros((ns * rows, nr * rows), F32)
        for q in range(ns):
            picked = jnp.dot(row_pick, cf[q].astype(BF16), preferred_element_type=F32).astype(BF16)
            plane_pick = (
                jnp.broadcast_to(plane_index, (nr * rows, tc))
                == lax.broadcasted_iota(jnp.int32, (nr * rows, tc), 1) + q * tc
            ).astype(F32).astype(BF16)
            total = total + lax.dot_general(
                picked, plane_pick, (((1,), (1,)), ((), ())), preferred_element_type=F32
            )
        kmat[...] = total.astype(BF16)

    halo_round = 1
    for number in range(ITERS):
        for c, e in blocks:
            deliver(halo_round, c, e, product(am, c, e), False)
        if number == 0:
            setup_middle()
            for c in range(per):
                loads_in[2 * per + c].wait()
                loads_in[3 * per + c].wait()
                combine(c, bm, bw)
            setup_end()
        for kind, c in everything:
            value = jnp.where(mask_of(kind, c), 0.5 * gathered(halo_round, kind, c), 0.0)
            if number == 0:
                iterate = step_sizes[0] * value
            else:
                value = value + momenta[number] * di[kind + c]
                iterate = mu[kind + c] + step_sizes[number] * value
            if number < ITERS - 1:
                di[kind + c] = value
                mu[kind + c] = iterate
            elif kind in (EAST, SOUTH):
                mult_out[0, c, 0 if kind == EAST else 1] = iterate
            put(kind, c, iterate)
        halo_round += 1

        for c in range(per):
            terms = jnp.dot(cpad[c], vec[c], preferred_element_type=F32).astype(BF16)
            ts[number, c * SLOT : (c + 1) * SLOT] = terms
            tp[number, pl.ds(r, 1), c * SLOT : (c + 1) * SLOT] = terms[None]
        tcopies = [
            peer_copy("sx", k, ts.at[number], tp.at[number, r], t_send.at[number], t_recv.at[number])
            for k in range(1, nr)
        ]
        for copy in tcopies:
            copy.start()
        for c, e in blocks:
            deliver(halo_round, c, e, product(bm, c, e), False)
        for copy in tcopies:
            copy.wait_recv()
        partial = jnp.dot(kmat[...], tp[number].reshape(nr * rows, 128), preferred_element_type=F32)
        ys[number] = partial.astype(BF16).reshape(ns, rows, 128)
        yr[number, pl.ds(s, 1)] = ys[number, pl.ds(s, 1)]
        ycopies = [
            peer_copy(
                "sy", k, ys.at[number, lax.rem(s + k, ns)], yr.at[number, s],
                y_send.at[number], y_recv.at[number],
            )
            for k in range(1, ns)
        ]
        for copy in ycopies:
            copy.start()
        for copy in ycopies:
            copy.wait_recv()
        solved = yr[number, 0].astype(F32)
        for q in range(1, ns):
            solved = solved + yr[number, q].astype(F32)
        solved = solved.astype(BF16)
        yo[number] = solved.reshape(per, SLOT, 128)
        for slot in all_slots:
            if_sending(slot, lambda to, slot=slot: solved_copy(number, slot, to).start())
        for c, e in blocks:
            loc[c, e * edge : (e + 1) * edge] = local_rows(c, e) + jnp.dot(
                ct[c, e * edge : (e + 1) * edge], solved[c * SLOT : (c + 1) * SLOT], preferred_element_type=F32
            )

        def across(slot):
            if_getting(slot, lambda to: solved_copy(number, slot, to).wait_recv())
            return jnp.dot(nct[slot], yn[number, slot], preferred_element_type=F32)

        for kind, c in everything:
            value = gathered(halo_round, kind, c)
            if kind == EAST and c == per - 1:
                value = value - across(FROM_RIGHT)
            elif kind == SOUTH:
                value = value - across(FROM_DOWN + c)
            elif kind == NORTH:
                value = value + across(FROM_UP + c)
            elif kind == WEST:
                value = value + across(FROM_LEFT)
            value = jnp.where(mask_of(kind, c), value, 0.0)
            put(kind, c, 0.5 * (ld[kind + c] - value))
        halo_round += 1
        for copy in tcopies + ycopies:
            copy.wait_send()

    for c, e in blocks:
        deliver(halo_round, c, e, product(am, c, e), True)
    for c in range(per):
        for kind in (EAST, SOUTH):
            value = jnp.where(mask_of(kind, c), 0.5 * gathered(halo_round, kind, c), 0.0)
            prec_out[0, c, 0 if kind == EAST else 1] = value

    for copy in cz + mzc + mxc + cx:
        copy.wait_send()
    for slot in all_slots:
        if_sending(slot, lambda to, slot=slot: coupling_copy(slot, to).wait_send())
        for number in range(ITERS):
            if_sending(slot, lambda to, slot=slot, number=number: solved_copy(number, slot, to).wait_send())
    down_right = [FROM_LEFT] + [FROM_UP + c for c in range(per)]
    up_left = [FROM_RIGHT] + [FROM_DOWN + c for c in range(per)]
    for k in range(halo_round + 1):
        slots = down_right if k == 0 else up_left if k == halo_round else down_right + up_left
        for slot in slots:
            left_behind(k, slot)


def hand_over(mult_ref, prec_ref, mult_out, prec_out):
    mult_out[...] = mult_ref[...]
    prec_out[...] = prec_ref[...]


def local(nr, ns, *args):
    adjoint_loads, dual_taut, coupling, coarse_inverse = args[0], args[1], args[5], args[6]
    per, edge, width = adjoint_loads.shape[1], adjoint_loads.shape[3], adjoint_loads.shape[4]
    size = dual_taut.shape[-1]
    tr, tc = coarse_inverse.shape
    rows = per * SLOT
    rounds = 2 * ITERS + 2
    slots = 2 + 2 * per
    meta_rows = rows + -(-2 * per // 8) * 8
    dma = pltpu.SemaphoreType.DMA
    vmem = pl.BlockSpec(memory_space=pltpu.VMEM)
    smem = pl.BlockSpec(memory_space=pltpu.SMEM)
    hbm = pl.BlockSpec(memory_space=pl.ANY)
    mats = [pltpu.VMEM((per, size, size), BF16)] * 4
    scratch = mats + [
        pltpu.VMEM((per, size, width), BF16),
        pltpu.VMEM((per, size, width), F32),
        pltpu.VMEM((rounds, slots, edge, width), BF16),
        pltpu.VMEM((rounds, slots, edge, width), BF16),
        pltpu.VMEM((3 * per + 1, edge, width), F32),
        pltpu.VMEM((3 * per + 1, edge, width), F32),
        pltpu.VMEM((3 * per + 1, edge, width), F32),
        pltpu.VMEM((per, SLOT, size), BF16),
        pltpu.VMEM((slots, SLOT, size), BF16),
        pltpu.VMEM((per, size, SLOT), BF16),
        pltpu.VMEM((slots, edge, SLOT), BF16),
        pltpu.VMEM((meta_rows, 128), jnp.int32),
        pltpu.VMEM((ns, meta_rows, 128), jnp.int32),
        pltpu.VMEM((nr, meta_rows, 128), jnp.int32),
        pltpu.VMEM((ns, nr * tr, tc), F32),
        pltpu.VMEM((ns * rows, nr * rows), BF16),
        pltpu.VMEM((ITERS, rows, width), BF16),
        pltpu.VMEM((ITERS, nr, rows, width), BF16),
        pltpu.VMEM((ITERS, ns, rows, width), BF16),
        pltpu.VMEM((ITERS, ns, rows, width), BF16),
        pltpu.VMEM((ITERS, per, SLOT, width), BF16),
        pltpu.VMEM((ITERS, slots, SLOT, width), BF16),
        dma((4 * per,)),
        dma((rounds, slots)), dma((rounds, slots)),
        dma((ns,)), dma((ns,)),
        dma((nr,)), dma((nr,)),
        dma((ns,)), dma((ns,)),
        dma((nr,)), dma((nr,)),
        dma((ITERS, nr)), dma((ITERS, nr)),
        dma((ITERS, ns)), dma((ITERS, ns)),
        dma((slots,)), dma((slots,)),
        dma((ITERS, slots)), dma((ITERS, slots)),
    ]
    out = jax.ShapeDtypeStruct(adjoint_loads.shape, F32)
    args = args[:5] + (jnp.transpose(coupling, (0, 2, 1, 3)),) + args[6:]
    results = pl.pallas_call(
        functools.partial(kernel, nr, ns),
        out_shape=(out, out),
        in_specs=[vmem, hbm, hbm, hbm, hbm, vmem, vmem, smem, smem, smem],
        out_specs=(vmem, vmem),
        scratch_shapes=scratch,
        compiler_params=pltpu.CompilerParams(
            collective_id=0, has_side_effects=True, vmem_limit_bytes=60 * 1024 * 1024
        ),
    )(*args)
    return pl.pallas_call(
        hand_over, out_shape=(out, out), in_specs=[vmem, vmem], out_specs=(vmem, vmem)
    )(*results)


def solution(mesh):
    placed = (
        P("sx", "sy", None, None, None),
        P("sx", "sy", None, None),
        P("sx", "sy", None, None),
        P("sx", "sy", None, None),
        P("sx", "sy", None, None),
        P("sx", "sy", None, None),
        P("sx", "sy"),
        P("sx", "sy"),
        P("sx", "sy", None),
        P("sx", "sy", None),
    )
    return jax.shard_map(
        functools.partial(local, mesh.shape["sx"], mesh.shape["sy"]),
        mesh=mesh,
        in_specs=placed,
        out_specs=(P("sx", "sy", None, None, None), P("sx", "sy", None, None, None)),
        check_vma=False,
    )
```

```python
import functools

import jax
import jax.numpy as jnp
from jax import lax
from jax.experimental import pallas as pl
from jax.experimental.pallas import tpu as pltpu
from jax.sharding import PartitionSpec as P

ITERS = 2
step_sizes = (0.55, 0.75)
momenta = (0.0, 0.15)

MESH = pl.DeviceIdType.MESH
SLOT = 16
F32 = jnp.float32
BF16 = jnp.bfloat16


def kernel(
    nr, ns,
    loads_ref, dual_t, dual_w, diri_t, diri_w, coup_ref, cinv_ref, wr_ref, len_ref, cm_ref,
    mult_out, prec_out,
    am, aw, bm, bw, vec, loc, snd, rcv, ld, mu, di, cpad, ncp, ct, nct, meta, mz, mx, cf, kmat, ts, tp, ys, yr, yo, yn,
    mat_sem, h_send, h_recv, mz_send, mz_recv, mx_send, mx_recv, cz_send, cz_recv, cx_send, cx_recv,
    t_send, t_recv, y_send, y_recv, c_send, c_recv, n_send, n_recv,
):
    r, s = lax.axis_index("sx"), lax.axis_index("sy")
    per = loads_ref.shape[1]
    edge, width = loads_ref.shape[3], loads_ref.shape[4]
    corners = coup_ref.shape[1]
    tr, tc = cinv_ref.shape
    order = nr * tr
    rows = per * SLOT
    has_left, has_right = s > 0, s < ns - 1
    has_up, has_down = r > 0, r < nr - 1
    FROM_LEFT, FROM_RIGHT, FROM_UP, FROM_DOWN = 0, 1, 2, 2 + per

    loads_in = []
    for i, (src, dst) in enumerate(((diri_t, am), (diri_w, aw), (dual_t, bm), (dual_w, bw))):
        for c in range(per):
            loads_in.append(pltpu.make_async_copy(src.at[0, c], dst.at[c], mat_sem.at[i * per + c]))
    for c in range(per):
        for i in (0, 1):
            loads_in[i * per + c].start()
    barrier = pltpu.get_barrier_semaphore()
    for k in range(1, nr):
        pl.semaphore_signal(barrier, inc=1, device_id={"sx": lax.rem(r + k, nr)}, device_id_type=MESH)
    for k in range(1, ns):
        pl.semaphore_signal(barrier, inc=1, device_id={"sy": lax.rem(s + k, ns)}, device_id_type=MESH)

    meta[...] = jnp.full(meta.shape, -1, jnp.int32)
    for c in range(per):
        for m in range(corners):
            meta[c * SLOT + m : c * SLOT + m + 1, :] = jnp.full((1, 128), cm_ref[0, c, m], jnp.int32)
        east = len_ref[0, c, 0]
        if c == per - 1:
            east = jnp.where(has_right, east, 0)
        south = jnp.where(has_down, len_ref[0, c, 1], 0)
        meta[rows + c : rows + c + 1, :] = jnp.full((1, 128), east, jnp.int32)
        meta[rows + per + c : rows + per + c + 1, :] = jnp.full((1, 128), south, jnp.int32)
    mz[pl.ds(s, 1)] = meta[...][None]
    mx[pl.ds(r, 1)] = meta[...][None]
    cf[pl.ds(s, 1), pl.ds(pl.multiple_of(r * tr, 8), tr), :] = cinv_ref[...].astype(F32)[None]

    positions = lax.broadcasted_iota(jnp.int32, (edge, width), 0)

    def live(length_row):
        return positions < jnp.broadcast_to(length_row, (edge, width))

    own_mask = {}
    for c in range(per):
        own_mask[c] = meta[rows + c : rows + c + 1, :]
        own_mask[per + c] = meta[rows + per + c : rows + per + c + 1, :]

    EAST, SOUTH, NORTH, WEST = 0, per, 2 * per, 3 * per

    def source_of(slot):
        if slot == FROM_LEFT:
            return per - 1
        if slot == FROM_RIGHT:
            return 0
        return slot - (FROM_UP if slot < FROM_DOWN else FROM_DOWN)

    def neighbour(src, dst, ssem, rsem, where_to):
        axis, shift = where_to
        index = (r if axis == "sx" else s) + shift
        return pltpu.make_async_remote_copy(
            src_ref=src, dst_ref=dst, send_sem=ssem, recv_sem=rsem,
            device_id={axis: index}, device_id_type=MESH,
        )

    def halo(k, slot, where_to):
        return neighbour(
            snd.at[k, slot], rcv.at[k, slot], h_send.at[k, slot], h_recv.at[k, slot], where_to
        )

    def coupling_copy(slot, where_to):
        return neighbour(cpad.at[source_of(slot)], ncp.at[slot], c_send.at[slot], c_recv.at[slot], where_to)

    def solved_copy(k, slot, where_to):
        return neighbour(
            yo.at[k, source_of(slot)], yn.at[k, slot], n_send.at[k, slot], n_recv.at[k, slot], where_to
        )

    def route(slot):
        if slot == FROM_LEFT:
            return ("sy", 1), has_right, has_left
        if slot == FROM_RIGHT:
            return ("sy", -1), has_left, has_right
        if slot < FROM_DOWN:
            return ("sx", 1), has_down, has_up
        return ("sx", -1), has_up, has_down

    all_slots = range(2 + 2 * per)

    def if_sending(slot, act):
        to, can, _ = route(slot)

        @pl.when(can)
        def _():
            act(to)

    def if_getting(slot, act):
        to, _, gets = route(slot)

        @pl.when(gets)
        def _():
            act(to)

    def send(k, slot, value):
        snd[k, slot] = value.astype(BF16)
        to, can, _ = route(slot)

        @pl.when(can)
        def _():
            halo(k, slot, to).start()

    def arrive(k, slot):
        to, _, gets = route(slot)

        @pl.when(gets)
        def _():
            halo(k, slot, to).wait_recv()

    def left_behind(k, slot):
        to, can, _ = route(slot)

        @pl.when(can)
        def _():
            halo(k, slot, to).wait_send()

    def put(kind, c, value):
        value = value.astype(BF16)
        if kind == EAST:
            vec[c, 0:edge] = value
            if c + 1 < per:
                vec[c + 1, 2 * edge : 3 * edge] = -value
        elif kind == SOUTH:
            vec[c, edge : 2 * edge] = value
        elif kind == NORTH:
            vec[c, 3 * edge :] = -value
        else:
            vec[0, 2 * edge : 3 * edge] = -value

    for c in range(per):
        for kind in (0, 1):
            e = kind * per + c
            value = jnp.where(live(own_mask[e]), loads_ref[0, c, kind], 0.0)
            ld[e] = value
            put(EAST if kind == 0 else SOUTH, c, 0.5 * value)
            if kind == 1:
                snd[0, FROM_UP + c] = value.astype(BF16)
            elif c == per - 1:
                snd[0, FROM_LEFT] = value.astype(BF16)
    pl.semaphore_wait(barrier, nr - 1 + ns - 1)
    for slot in [FROM_LEFT] + [FROM_UP + c for c in range(per)]:
        to, can, _ = route(slot)

        @pl.when(can)
        def _(to=to, slot=slot):
            halo(0, slot, to).start()

    def peer_copy(axis, k, src, dst, ssem, rsem):
        n, me = (nr, r) if axis == "sx" else (ns, s)
        return pltpu.make_async_remote_copy(
            src_ref=src, dst_ref=dst, send_sem=ssem.at[k], recv_sem=rsem.at[k],
            device_id={axis: lax.rem(me + k, n)}, device_id_type=MESH,
        )

    my_rows = pl.ds(pl.multiple_of(r * tr, 8), tr)
    cz = [peer_copy("sy", k, cf.at[s, my_rows], cf.at[s, my_rows], cz_send, cz_recv) for k in range(1, ns)]
    mzc = [peer_copy("sy", k, meta, mz.at[s], mz_send, mz_recv) for k in range(1, ns)]
    mxc = [peer_copy("sx", k, meta, mx.at[r], mx_send, mx_recv) for k in range(1, nr)]
    cx = [peer_copy("sx", k, cf.at[:, my_rows], cf.at[:, my_rows], cx_send, cx_recv) for k in range(1, nr)]
    for copy in cz + mzc + mxc:
        copy.start()

    cpad[...] = jnp.zeros(cpad.shape, BF16)
    for c in range(per):
        cpad[c, 0:corners] = coup_ref[0, :, c, :]

    for slot in all_slots:
        if_sending(slot, lambda to, slot=slot: coupling_copy(slot, to).start())

    def combine(c, main, extra):
        flag = jnp.full((1, 1), wr_ref[0, c], jnp.int32).astype(F32).astype(BF16)
        size = main.shape[1]
        step = 128

        def body(i, _):
            part = pl.ds(pl.multiple_of(i * step, step), step)
            main[c, part] = main[c, part] + flag * extra[c, part]
            return 0

        lax.fori_loop(0, size // step, body, 0)

    def product(mat, c, e):
        return jnp.dot(mat[c, e * edge : (e + 1) * edge, :], vec[c], preferred_element_type=F32)

    blocks = [(c, 3) for c in range(per)] + [(c, 1) for c in range(per)]
    blocks += [(per - 1, 0), (0, 2)]
    blocks += [(c, 0) for c in range(per - 1)] + [(c, 2) for c in range(1, per)]

    def slot_of(c, e):
        if e == 3:
            return FROM_DOWN + c
        if e == 1:
            return FROM_UP + c
        if e == 0 and c == per - 1:
            return FROM_LEFT
        if e == 2 and c == 0:
            return FROM_RIGHT
        return None

    def deliver(k, c, e, value, last):
        loc[c, e * edge : (e + 1) * edge] = value
        slot = slot_of(c, e)
        if slot is not None and not (last and e in (0, 1)):
            send(k, slot, value)

    def local_rows(c, e):
        return loc[c, e * edge : (e + 1) * edge]

    def mask_of(kind, c):
        if kind == EAST:
            return live(own_mask[c])
        if kind == SOUTH:
            return live(own_mask[per + c])
        if kind == NORTH:
            row = mx[jnp.maximum(r - 1, 0), rows + per + c : rows + per + c + 1, :]
            return live(jnp.where(has_up, row, 0))
        row = mz[jnp.maximum(s - 1, 0), rows + per - 1 : rows + per, :]
        return live(jnp.where(has_left, row, 0))

    def gathered(k, kind, c):
        if kind == EAST:
            if c + 1 < per:
                return local_rows(c, 0) - local_rows(c + 1, 2)
            arrive(k, FROM_RIGHT)
            return local_rows(c, 0) - rcv[k, FROM_RIGHT].astype(F32)
        if kind == SOUTH:
            arrive(k, FROM_DOWN + c)
            return local_rows(c, 1) - rcv[k, FROM_DOWN + c].astype(F32)
        if kind == NORTH:
            arrive(k, FROM_UP + c)
            return rcv[k, FROM_UP + c].astype(F32) - local_rows(c, 3)
        arrive(k, FROM_LEFT)
        return rcv[k, FROM_LEFT].astype(F32) - local_rows(0, 2)

    inner = [(EAST, c) for c in range(per)]
    everything = inner + [(WEST, 0)] + [(SOUTH, c) for c in range(per)] + [(NORTH, c) for c in range(per)]

    for c in range(per):
        loads_in[c].wait()
        loads_in[per + c].wait()
        loads_in[2 * per + c].start()
        loads_in[3 * per + c].start()
        combine(c, am, aw)
    for slot, kind, c, there in [(FROM_LEFT, WEST, 0, has_left)] + [(FROM_UP + c, NORTH, c, has_up) for c in range(per)]:
        arrive(0, slot)
        value = jnp.where(jnp.broadcast_to(there, (edge, width)), rcv[0, slot].astype(F32), 0.0)
        ld[kind + c] = value
        put(kind, c, 0.5 * value)

    def setup_middle():
        for k in range(ns - 1):
            cz[k].wait_recv()
            mzc[k].wait_recv()
        for copy in cx:
            copy.start()
        for k in range(nr - 1):
            mxc[k].wait_recv()

    def setup_coupling():
        for c in range(per):
            ct[c] = cpad[c].astype(F32).T.astype(BF16)
        for slot in all_slots:
            if_getting(slot, lambda to, slot=slot: coupling_copy(slot, to).wait_recv())
            e = 0 if slot == FROM_LEFT else 2 if slot == FROM_RIGHT else 1 if slot < FROM_DOWN else 3
            nct[slot] = ncp[slot].astype(F32).T[e * edge : (e + 1) * edge].astype(BF16)

    def setup_coarse():
        for k in range(nr - 1):
            cx[k].wait_recv()
        row_index = mz[:, 0:rows, :].reshape(ns * rows, 128)[:, 0:1]
        plane_index = mx[:, 0:rows, :].reshape(nr * rows, 128)[:, 0:1]
        row_pick = (
            jnp.broadcast_to(row_index, (ns * rows, order))
            == lax.broadcasted_iota(jnp.int32, (ns * rows, order), 1)
        ).astype(F32).astype(BF16)
        total = jnp.zeros((ns * rows, nr * rows), F32)
        for q in range(ns):
            picked = jnp.dot(row_pick, cf[q].astype(BF16), preferred_element_type=F32).astype(BF16)
            plane_pick = (
                jnp.broadcast_to(plane_index, (nr * rows, tc))
                == lax.broadcasted_iota(jnp.int32, (nr * rows, tc), 1) + q * tc
            ).astype(F32).astype(BF16)
            total = total + lax.dot_general(
                picked, plane_pick, (((1,), (1,)), ((), ())), preferred_element_type=F32
            )
        kmat[...] = total.astype(BF16)

    halo_round = 1
    for number in range(ITERS):
        for c, e in blocks:
            deliver(halo_round, c, e, product(am, c, e), False)
        if number == 0:
            setup_middle()
            for c in range(per):
                loads_in[2 * per + c].wait()
                loads_in[3 * per + c].wait()
                combine(c, bm, bw)
        for kind, c in everything:
            value = jnp.where(mask_of(kind, c), 0.5 * gathered(halo_round, kind, c), 0.0)
            if number == 0:
                iterate = step_sizes[0] * value
            else:
                value = value + momenta[number] * di[kind + c]
                iterate = mu[kind + c] + step_sizes[number] * value
            if number < ITERS - 1:
                di[kind + c] = value
                mu[kind + c] = iterate
            elif kind in (EAST, SOUTH):
                mult_out[0, c, 0 if kind == EAST else 1] = iterate
            put(kind, c, iterate)
        halo_round += 1

        for c in range(per):
            terms = jnp.dot(cpad[c], vec[c], preferred_element_type=F32).astype(BF16)
            ts[number, c * SLOT : (c + 1) * SLOT] = terms
            tp[number, pl.ds(r, 1), c * SLOT : (c + 1) * SLOT] = terms[None]
        tcopies = [
            peer_copy("sx", k, ts.at[number], tp.at[number, r], t_send.at[number], t_recv.at[number])
            for k in range(1, nr)
        ]
        for copy in tcopies:
            copy.start()
        for c, e in blocks:
            value = product(bm, c, e)
            loc[c, e * edge : (e + 1) * edge] = value
            if slot_of(c, e) is not None:
                snd[halo_round, slot_of(c, e)] = value.astype(BF16)
        if number == 0:
            setup_coarse()
        for copy in tcopies:
            copy.wait_recv()
        partial = jnp.dot(kmat[...], tp[number].reshape(nr * rows, 128), preferred_element_type=F32)
        ys[number] = partial.astype(BF16).reshape(ns, rows, 128)
        yr[number, pl.ds(s, 1)] = ys[number, pl.ds(s, 1)]
        ycopies = [
            peer_copy(
                "sy", k, ys.at[number, lax.rem(s + k, ns)], yr.at[number, s],
                y_send.at[number], y_recv.at[number],
            )
            for k in range(1, ns)
        ]
        for copy in ycopies:
            copy.start()
        for c, e in blocks:
            slot = slot_of(c, e)
            if slot is not None:
                if_sending(slot, lambda to, slot=slot: halo(halo_round, slot, to).start())
        if number == 0:
            setup_coupling()
        for copy in ycopies:
            copy.wait_recv()
        solved = yr[number, 0].astype(F32)
        for q in range(1, ns):
            solved = solved + yr[number, q].astype(F32)
        solved = solved.astype(BF16)
        yo[number] = solved.reshape(per, SLOT, 128)
        for slot in all_slots:
            if_sending(slot, lambda to, slot=slot: solved_copy(number, slot, to).start())
        for c, e in blocks:
            loc[c, e * edge : (e + 1) * edge] = local_rows(c, e) + jnp.dot(
                ct[c, e * edge : (e + 1) * edge], solved[c * SLOT : (c + 1) * SLOT], preferred_element_type=F32
            )

        def across(slot):
            if_getting(slot, lambda to: solved_copy(number, slot, to).wait_recv())
            return jnp.dot(nct[slot], yn[number, slot], preferred_element_type=F32)

        for kind, c in everything:
            value = gathered(halo_round, kind, c)
            if kind == EAST and c == per - 1:
                value = value - across(FROM_RIGHT)
            elif kind == SOUTH:
                value = value - across(FROM_DOWN + c)
            elif kind == NORTH:
                value = value + across(FROM_UP + c)
            elif kind == WEST:
                value = value + across(FROM_LEFT)
            value = jnp.where(mask_of(kind, c), value, 0.0)
            put(kind, c, 0.5 * (ld[kind + c] - value))
        halo_round += 1
        for copy in tcopies + ycopies:
            copy.wait_send()

    for c, e in blocks:
        deliver(halo_round, c, e, product(am, c, e), True)
    for c in range(per):
        for kind in (EAST, SOUTH):
            value = jnp.where(mask_of(kind, c), 0.5 * gathered(halo_round, kind, c), 0.0)
            prec_out[0, c, 0 if kind == EAST else 1] = value

    for copy in cz + mzc + mxc + cx:
        copy.wait_send()
    for slot in all_slots:
        if_sending(slot, lambda to, slot=slot: coupling_copy(slot, to).wait_send())
        for number in range(ITERS):
            if_sending(slot, lambda to, slot=slot, number=number: solved_copy(number, slot, to).wait_send())
    down_right = [FROM_LEFT] + [FROM_UP + c for c in range(per)]
    up_left = [FROM_RIGHT] + [FROM_DOWN + c for c in range(per)]
    for k in range(halo_round + 1):
        slots = down_right if k == 0 else up_left if k == halo_round else down_right + up_left
        for slot in slots:
            left_behind(k, slot)


def hand_over(mult_ref, prec_ref, mult_out, prec_out):
    mult_out[...] = mult_ref[...]
    prec_out[...] = prec_ref[...]


def local(nr, ns, *args):
    adjoint_loads, dual_taut, coupling, coarse_inverse = args[0], args[1], args[5], args[6]
    per, edge, width = adjoint_loads.shape[1], adjoint_loads.shape[3], adjoint_loads.shape[4]
    size = dual_taut.shape[-1]
    tr, tc = coarse_inverse.shape
    rows = per * SLOT
    rounds = 2 * ITERS + 2
    slots = 2 + 2 * per
    meta_rows = rows + -(-2 * per // 8) * 8
    dma = pltpu.SemaphoreType.DMA
    vmem = pl.BlockSpec(memory_space=pltpu.VMEM)
    smem = pl.BlockSpec(memory_space=pltpu.SMEM)
    hbm = pl.BlockSpec(memory_space=pl.ANY)
    mats = [pltpu.VMEM((per, size, size), BF16)] * 4
    scratch = mats + [
        pltpu.VMEM((per, size, width), BF16),
        pltpu.VMEM((per, size, width), F32),
        pltpu.VMEM((rounds, slots, edge, width), BF16),
        pltpu.VMEM((rounds, slots, edge, width), BF16),
        pltpu.VMEM((3 * per + 1, edge, width), F32),
        pltpu.VMEM((3 * per + 1, edge, width), F32),
        pltpu.VMEM((3 * per + 1, edge, width), F32),
        pltpu.VMEM((per, SLOT, size), BF16),
        pltpu.VMEM((slots, SLOT, size), BF16),
        pltpu.VMEM((per, size, SLOT), BF16),
        pltpu.VMEM((slots, edge, SLOT), BF16),
        pltpu.VMEM((meta_rows, 128), jnp.int32),
        pltpu.VMEM((ns, meta_rows, 128), jnp.int32),
        pltpu.VMEM((nr, meta_rows, 128), jnp.int32),
        pltpu.VMEM((ns, nr * tr, tc), F32),
        pltpu.VMEM((ns * rows, nr * rows), BF16),
        pltpu.VMEM((ITERS, rows, width), BF16),
        pltpu.VMEM((ITERS, nr, rows, width), BF16),
        pltpu.VMEM((ITERS, ns, rows, width), BF16),
        pltpu.VMEM((ITERS, ns, rows, width), BF16),
        pltpu.VMEM((ITERS, per, SLOT, width), BF16),
        pltpu.VMEM((ITERS, slots, SLOT, width), BF16),
        dma((4 * per,)),
        dma((rounds, slots)), dma((rounds, slots)),
        dma((ns,)), dma((ns,)),
        dma((nr,)), dma((nr,)),
        dma((ns,)), dma((ns,)),
        dma((nr,)), dma((nr,)),
        dma((ITERS, nr)), dma((ITERS, nr)),
        dma((ITERS, ns)), dma((ITERS, ns)),
        dma((slots,)), dma((slots,)),
        dma((ITERS, slots)), dma((ITERS, slots)),
    ]
    out = jax.ShapeDtypeStruct(adjoint_loads.shape, F32)
    args = args[:5] + (jnp.transpose(coupling, (0, 2, 1, 3)),) + args[6:]
    results = pl.pallas_call(
        functools.partial(kernel, nr, ns),
        out_shape=(out, out),
        in_specs=[vmem, hbm, hbm, hbm, hbm, vmem, vmem, smem, smem, smem],
        out_specs=(vmem, vmem),
        scratch_shapes=scratch,
        compiler_params=pltpu.CompilerParams(
            collective_id=0, has_side_effects=True, vmem_limit_bytes=60 * 1024 * 1024
        ),
    )(*args)
    return pl.pallas_call(
        hand_over, out_shape=(out, out), in_specs=[vmem, vmem], out_specs=(vmem, vmem)
    )(*results)


def solution(mesh):
    placed = (
        P("sx", "sy", None, None, None),
        P("sx", "sy", None, None),
        P("sx", "sy", None, None),
        P("sx", "sy", None, None),
        P("sx", "sy", None, None),
        P("sx", "sy", None, None),
        P("sx", "sy"),
        P("sx", "sy"),
        P("sx", "sy", None),
        P("sx", "sy", None),
    )
    return jax.shard_map(
        functools.partial(local, mesh.shape["sx"], mesh.shape["sy"]),
        mesh=mesh,
        in_specs=placed,
        out_specs=(P("sx", "sy", None, None, None), P("sx", "sy", None, None, None)),
        check_vma=False,
    )
```

```python
import functools

import jax
import jax.numpy as jnp
from jax import lax
from jax.experimental import pallas as pl
from jax.experimental.pallas import tpu as pltpu
from jax.sharding import PartitionSpec as P

ITERS = 2
step_sizes = (0.55, 0.75)
momenta = (0.0, 0.15)

MESH = pl.DeviceIdType.MESH
SLOT = 16
F32 = jnp.float32
BF16 = jnp.bfloat16


def kernel(
    nr, ns,
    loads_ref, dual_t, dual_w, diri_t, diri_w, coup_ref, cinv_ref, wr_ref, len_ref, cm_ref,
    mult_out, prec_out,
    am, aw, bm, bw, vec, loc, snd, rcv, ld, mu, di, cpad, ncp, ct, nct, meta, mz, mx, cf, kmat, ts, tp, ys, yr, yo, yn,
    mat_sem, h_send, h_recv, mz_send, mz_recv, mx_send, mx_recv, cz_send, cz_recv, cx_send, cx_recv,
    t_send, t_recv, y_send, y_recv, c_send, c_recv, n_send, n_recv,
):
    r, s = lax.axis_index("sx"), lax.axis_index("sy")
    per = loads_ref.shape[1]
    edge, width = loads_ref.shape[3], loads_ref.shape[4]
    corners = coup_ref.shape[1]
    tr, tc = cinv_ref.shape
    order = nr * tr
    rows = per * SLOT
    has_left, has_right = s > 0, s < ns - 1
    has_up, has_down = r > 0, r < nr - 1
    FROM_LEFT, FROM_RIGHT, FROM_UP, FROM_DOWN = 0, 1, 2, 2 + per

    loads_in = []
    for i, (src, dst) in enumerate(((diri_t, am), (diri_w, aw), (dual_t, bm), (dual_w, bw))):
        for c in range(per):
            loads_in.append(pltpu.make_async_copy(src.at[0, c], dst.at[c], mat_sem.at[i * per + c]))
    for c in range(per):
        for i in (0, 1):
            loads_in[i * per + c].start()
    barrier = pltpu.get_barrier_semaphore()
    for k in range(1, nr):
        pl.semaphore_signal(barrier, inc=1, device_id={"sx": lax.rem(r + k, nr)}, device_id_type=MESH)
    for k in range(1, ns):
        pl.semaphore_signal(barrier, inc=1, device_id={"sy": lax.rem(s + k, ns)}, device_id_type=MESH)

    meta[...] = jnp.full(meta.shape, -1, jnp.int32)
    for c in range(per):
        for m in range(corners):
            meta[c * SLOT + m : c * SLOT + m + 1, :] = jnp.full((1, 128), cm_ref[0, c, m], jnp.int32)
        east = len_ref[0, c, 0]
        if c == per - 1:
            east = jnp.where(has_right, east, 0)
        south = jnp.where(has_down, len_ref[0, c, 1], 0)
        meta[rows + c : rows + c + 1, :] = jnp.full((1, 128), east, jnp.int32)
        meta[rows + per + c : rows + per + c + 1, :] = jnp.full((1, 128), south, jnp.int32)
    mz[pl.ds(s, 1)] = meta[...][None]
    mx[pl.ds(r, 1)] = meta[...][None]
    cf[pl.ds(s, 1), pl.ds(pl.multiple_of(r * tr, 8), tr), :] = cinv_ref[...].astype(F32)[None]

    positions = lax.broadcasted_iota(jnp.int32, (edge, width), 0)

    def live(length_row):
        return positions < jnp.broadcast_to(length_row, (edge, width))

    own_mask = {}
    for c in range(per):
        own_mask[c] = meta[rows + c : rows + c + 1, :]
        own_mask[per + c] = meta[rows + per + c : rows + per + c + 1, :]

    EAST, SOUTH, NORTH, WEST = 0, per, 2 * per, 3 * per

    def source_of(slot):
        if slot == FROM_LEFT:
            return per - 1
        if slot == FROM_RIGHT:
            return 0
        return slot - (FROM_UP if slot < FROM_DOWN else FROM_DOWN)

    def neighbour(src, dst, ssem, rsem, where_to):
        axis, shift = where_to
        index = (r if axis == "sx" else s) + shift
        return pltpu.make_async_remote_copy(
            src_ref=src, dst_ref=dst, send_sem=ssem, recv_sem=rsem,
            device_id={axis: index}, device_id_type=MESH,
        )

    def halo(k, slot, where_to):
        return neighbour(
            snd.at[k, slot], rcv.at[k, slot], h_send.at[k, slot], h_recv.at[k, slot], where_to
        )

    def coupling_copy(slot, where_to):
        return neighbour(cpad.at[source_of(slot)], ncp.at[slot], c_send.at[slot], c_recv.at[slot], where_to)

    def solved_copy(k, slot, where_to):
        return neighbour(
            yo.at[k, source_of(slot)], yn.at[k, slot], n_send.at[k, slot], n_recv.at[k, slot], where_to
        )

    def route(slot):
        if slot == FROM_LEFT:
            return ("sy", 1), has_right, has_left
        if slot == FROM_RIGHT:
            return ("sy", -1), has_left, has_right
        if slot < FROM_DOWN:
            return ("sx", 1), has_down, has_up
        return ("sx", -1), has_up, has_down

    all_slots = range(2 + 2 * per)

    def if_sending(slot, act):
        to, can, _ = route(slot)

        @pl.when(can)
        def _():
            act(to)

    def if_getting(slot, act):
        to, _, gets = route(slot)

        @pl.when(gets)
        def _():
            act(to)

    def send(k, slot, value):
        snd[k, slot] = value.astype(BF16)
        to, can, _ = route(slot)

        @pl.when(can)
        def _():
            halo(k, slot, to).start()

    def arrive(k, slot):
        to, _, gets = route(slot)

        @pl.when(gets)
        def _():
            halo(k, slot, to).wait_recv()

    def left_behind(k, slot):
        to, can, _ = route(slot)

        @pl.when(can)
        def _():
            halo(k, slot, to).wait_send()

    def put(kind, c, value):
        value = value.astype(BF16)
        if kind == EAST:
            vec[c, 0:edge] = value
            if c + 1 < per:
                vec[c + 1, 2 * edge : 3 * edge] = -value
        elif kind == SOUTH:
            vec[c, edge : 2 * edge] = value
        elif kind == NORTH:
            vec[c, 3 * edge :] = -value
        else:
            vec[0, 2 * edge : 3 * edge] = -value

    for c in range(per):
        for kind in (0, 1):
            e = kind * per + c
            value = jnp.where(live(own_mask[e]), loads_ref[0, c, kind], 0.0)
            ld[e] = value
            put(EAST if kind == 0 else SOUTH, c, 0.5 * value)
            if kind == 1:
                snd[0, FROM_UP + c] = value.astype(BF16)
            elif c == per - 1:
                snd[0, FROM_LEFT] = value.astype(BF16)
    pl.semaphore_wait(barrier, nr - 1 + ns - 1)
    for slot in [FROM_LEFT] + [FROM_UP + c for c in range(per)]:
        to, can, _ = route(slot)

        @pl.when(can)
        def _(to=to, slot=slot):
            halo(0, slot, to).start()

    def peer_copy(axis, k, src, dst, ssem, rsem):
        n, me = (nr, r) if axis == "sx" else (ns, s)
        return pltpu.make_async_remote_copy(
            src_ref=src, dst_ref=dst, send_sem=ssem.at[k], recv_sem=rsem.at[k],
            device_id={axis: lax.rem(me + k, n)}, device_id_type=MESH,
        )

    my_rows = pl.ds(pl.multiple_of(r * tr, 8), tr)
    cz = [peer_copy("sy", k, cf.at[s, my_rows], cf.at[s, my_rows], cz_send, cz_recv) for k in range(1, ns)]
    mzc = [peer_copy("sy", k, meta, mz.at[s], mz_send, mz_recv) for k in range(1, ns)]
    mxc = [peer_copy("sx", k, meta, mx.at[r], mx_send, mx_recv) for k in range(1, nr)]
    cx = [peer_copy("sx", k, cf.at[:, my_rows], cf.at[:, my_rows], cx_send, cx_recv) for k in range(1, nr)]
    for copy in cz + mzc + mxc:
        copy.start()

    cpad[...] = jnp.zeros(cpad.shape, BF16)
    for c in range(per):
        cpad[c, 0:corners] = coup_ref[0, :, c, :]

    for slot in all_slots:
        if_sending(slot, lambda to, slot=slot: coupling_copy(slot, to).start())

    def combine(c, main, extra):
        flag = jnp.full((1, 1), wr_ref[0, c], jnp.int32).astype(F32).astype(BF16)
        size = main.shape[1]
        step = 128

        def body(i, _):
            part = pl.ds(pl.multiple_of(i * step, step), step)
            main[c, part] = main[c, part] + flag * extra[c, part]
            return 0

        lax.fori_loop(0, size // step, body, 0)

    def product(mat, c, e):
        return jnp.dot(mat[c, e * edge : (e + 1) * edge, :], vec[c], preferred_element_type=F32)

    blocks = [(c, 3) for c in range(per)] + [(c, 1) for c in range(per)]
    blocks += [(per - 1, 0), (0, 2)]
    blocks += [(c, 0) for c in range(per - 1)] + [(c, 2) for c in range(1, per)]

    def slot_of(c, e):
        if e == 3:
            return FROM_DOWN + c
        if e == 1:
            return FROM_UP + c
        if e == 0 and c == per - 1:
            return FROM_LEFT
        if e == 2 and c == 0:
            return FROM_RIGHT
        return None

    def deliver(k, c, e, value, last):
        loc[c, e * edge : (e + 1) * edge] = value
        slot = slot_of(c, e)
        if slot is not None and not (last and e in (0, 1)):
            send(k, slot, value)

    def local_rows(c, e):
        return loc[c, e * edge : (e + 1) * edge]

    def mask_of(kind, c):
        if kind == EAST:
            return live(own_mask[c])
        if kind == SOUTH:
            return live(own_mask[per + c])
        if kind == NORTH:
            row = mx[jnp.maximum(r - 1, 0), rows + per + c : rows + per + c + 1, :]
            return live(jnp.where(has_up, row, 0))
        row = mz[jnp.maximum(s - 1, 0), rows + per - 1 : rows + per, :]
        return live(jnp.where(has_left, row, 0))

    def gathered(k, kind, c):
        if kind == EAST:
            if c + 1 < per:
                return local_rows(c, 0) - local_rows(c + 1, 2)
            arrive(k, FROM_RIGHT)
            return local_rows(c, 0) - rcv[k, FROM_RIGHT].astype(F32)
        if kind == SOUTH:
            arrive(k, FROM_DOWN + c)
            return local_rows(c, 1) - rcv[k, FROM_DOWN + c].astype(F32)
        if kind == NORTH:
            arrive(k, FROM_UP + c)
            return rcv[k, FROM_UP + c].astype(F32) - local_rows(c, 3)
        arrive(k, FROM_LEFT)
        return rcv[k, FROM_LEFT].astype(F32) - local_rows(0, 2)

    inner = [(EAST, c) for c in range(per)]
    everything = inner + [(WEST, 0)] + [(SOUTH, c) for c in range(per)] + [(NORTH, c) for c in range(per)]

    for c in range(per):
        loads_in[c].wait()
        loads_in[per + c].wait()
        loads_in[2 * per + c].start()
        loads_in[3 * per + c].start()
        combine(c, am, aw)
    for slot, kind, c, there in [(FROM_LEFT, WEST, 0, has_left)] + [(FROM_UP + c, NORTH, c, has_up) for c in range(per)]:
        arrive(0, slot)
        value = jnp.where(jnp.broadcast_to(there, (edge, width)), rcv[0, slot].astype(F32), 0.0)
        ld[kind + c] = value
        put(kind, c, 0.5 * value)

    def setup_middle():
        for k in range(ns - 1):
            cz[k].wait_recv()
            mzc[k].wait_recv()
        for copy in cx:
            copy.start()
        for k in range(nr - 1):
            mxc[k].wait_recv()

    def setup_coupling():
        for c in range(per):
            ct[c] = cpad[c].astype(F32).T.astype(BF16)
        for slot in all_slots:
            if_getting(slot, lambda to, slot=slot: coupling_copy(slot, to).wait_recv())
            e = 0 if slot == FROM_LEFT else 2 if slot == FROM_RIGHT else 1 if slot < FROM_DOWN else 3
            nct[slot] = ncp[slot].astype(F32).T[e * edge : (e + 1) * edge].astype(BF16)

    def setup_coarse():
        for k in range(nr - 1):
            cx[k].wait_recv()
        row_index = mz[:, 0:rows, :].reshape(ns * rows, 128)[:, 0:1]
        plane_index = mx[:, 0:rows, :].reshape(nr * rows, 128)[:, 0:1]
        row_pick = (
            jnp.broadcast_to(row_index, (ns * rows, order))
            == lax.broadcasted_iota(jnp.int32, (ns * rows, order), 1)
        ).astype(F32).astype(BF16)
        total = jnp.zeros((ns * rows, nr * rows), F32)
        for q in range(ns):
            picked = jnp.dot(row_pick, cf[q].astype(BF16), preferred_element_type=F32).astype(BF16)
            plane_pick = (
                jnp.broadcast_to(plane_index, (nr * rows, tc))
                == lax.broadcasted_iota(jnp.int32, (nr * rows, tc), 1) + q * tc
            ).astype(F32).astype(BF16)
            total = total + lax.dot_general(
                picked, plane_pick, (((1,), (1,)), ((), ())), preferred_element_type=F32
            )
        kmat[...] = total.astype(BF16)

    halo_round = 1
    for number in range(ITERS):
        for c, e in blocks:
            deliver(halo_round, c, e, product(am, c, e), False)
        if number == 0:
            setup_middle()
            for c in range(per):
                loads_in[2 * per + c].wait()
                loads_in[3 * per + c].wait()
                combine(c, bm, bw)
        for kind, c in everything:
            value = jnp.where(mask_of(kind, c), 0.5 * gathered(halo_round, kind, c), 0.0)
            if number == 0:
                iterate = step_sizes[0] * value
            else:
                value = value + momenta[number] * di[kind + c]
                iterate = mu[kind + c] + step_sizes[number] * value
            if number < ITERS - 1:
                di[kind + c] = value
                mu[kind + c] = iterate
            elif kind in (EAST, SOUTH):
                mult_out[0, c, 0 if kind == EAST else 1] = iterate
            put(kind, c, iterate)
        halo_round += 1

        for c in range(per):
            terms = jnp.dot(cpad[c], vec[c], preferred_element_type=F32).astype(BF16)
            ts[number, c * SLOT : (c + 1) * SLOT] = terms
            tp[number, pl.ds(r, 1), c * SLOT : (c + 1) * SLOT] = terms[None]
        tcopies = [
            peer_copy("sx", k, ts.at[number], tp.at[number, r], t_send.at[number], t_recv.at[number])
            for k in range(1, nr)
        ]
        for copy in tcopies:
            copy.start()
        for c, e in blocks:
            value = product(bm, c, e)
            loc[c, e * edge : (e + 1) * edge] = value
            if slot_of(c, e) is not None:
                snd[halo_round, slot_of(c, e)] = value.astype(BF16)
                if e in (1, 3):
                    if_sending(slot_of(c, e), lambda to, slot=slot_of(c, e): halo(halo_round, slot, to).start())
        if number == 0:
            setup_coarse()
        for copy in tcopies:
            copy.wait_recv()
        partial = jnp.dot(kmat[...], tp[number].reshape(nr * rows, 128), preferred_element_type=F32)
        ys[number] = partial.astype(BF16).reshape(ns, rows, 128)
        yr[number, pl.ds(s, 1)] = ys[number, pl.ds(s, 1)]
        ycopies = [
            peer_copy(
                "sy", k, ys.at[number, lax.rem(s + k, ns)], yr.at[number, s],
                y_send.at[number], y_recv.at[number],
            )
            for k in range(1, ns)
        ]
        for copy in ycopies:
            copy.start()
        for c, e in blocks:
            slot = slot_of(c, e)
            if slot is not None and e in (0, 2):
                if_sending(slot, lambda to, slot=slot: halo(halo_round, slot, to).start())
        if number == 0:
            setup_coupling()
        for copy in ycopies:
            copy.wait_recv()
        solved = yr[number, 0].astype(F32)
        for q in range(1, ns):
            solved = solved + yr[number, q].astype(F32)
        solved = solved.astype(BF16)
        yo[number] = solved.reshape(per, SLOT, 128)
        for slot in all_slots:
            if_sending(slot, lambda to, slot=slot: solved_copy(number, slot, to).start())
        for c, e in blocks:
            loc[c, e * edge : (e + 1) * edge] = local_rows(c, e) + jnp.dot(
                ct[c, e * edge : (e + 1) * edge], solved[c * SLOT : (c + 1) * SLOT], preferred_element_type=F32
            )

        def across(slot):
            if_getting(slot, lambda to: solved_copy(number, slot, to).wait_recv())
            return jnp.dot(nct[slot], yn[number, slot], preferred_element_type=F32)

        for kind, c in everything:
            value = gathered(halo_round, kind, c)
            if kind == EAST and c == per - 1:
                value = value - across(FROM_RIGHT)
            elif kind == SOUTH:
                value = value - across(FROM_DOWN + c)
            elif kind == NORTH:
                value = value + across(FROM_UP + c)
            elif kind == WEST:
                value = value + across(FROM_LEFT)
            value = jnp.where(mask_of(kind, c), value, 0.0)
            put(kind, c, 0.5 * (ld[kind + c] - value))
        halo_round += 1
        for copy in tcopies + ycopies:
            copy.wait_send()

    for c, e in blocks:
        deliver(halo_round, c, e, product(am, c, e), True)
    for c in range(per):
        for kind in (EAST, SOUTH):
            value = jnp.where(mask_of(kind, c), 0.5 * gathered(halo_round, kind, c), 0.0)
            prec_out[0, c, 0 if kind == EAST else 1] = value

    for copy in cz + mzc + mxc + cx:
        copy.wait_send()
    for slot in all_slots:
        if_sending(slot, lambda to, slot=slot: coupling_copy(slot, to).wait_send())
        for number in range(ITERS):
            if_sending(slot, lambda to, slot=slot, number=number: solved_copy(number, slot, to).wait_send())
    down_right = [FROM_LEFT] + [FROM_UP + c for c in range(per)]
    up_left = [FROM_RIGHT] + [FROM_DOWN + c for c in range(per)]
    for k in range(halo_round + 1):
        slots = down_right if k == 0 else up_left if k == halo_round else down_right + up_left
        for slot in slots:
            left_behind(k, slot)


def hand_over(mult_ref, prec_ref, mult_out, prec_out):
    mult_out[...] = mult_ref[...]
    prec_out[...] = prec_ref[...]


def local(nr, ns, *args):
    adjoint_loads, dual_taut, coupling, coarse_inverse = args[0], args[1], args[5], args[6]
    per, edge, width = adjoint_loads.shape[1], adjoint_loads.shape[3], adjoint_loads.shape[4]
    size = dual_taut.shape[-1]
    tr, tc = coarse_inverse.shape
    rows = per * SLOT
    rounds = 2 * ITERS + 2
    slots = 2 + 2 * per
    meta_rows = rows + -(-2 * per // 8) * 8
    dma = pltpu.SemaphoreType.DMA
    vmem = pl.BlockSpec(memory_space=pltpu.VMEM)
    smem = pl.BlockSpec(memory_space=pltpu.SMEM)
    hbm = pl.BlockSpec(memory_space=pl.ANY)
    mats = [pltpu.VMEM((per, size, size), BF16)] * 4
    scratch = mats + [
        pltpu.VMEM((per, size, width), BF16),
        pltpu.VMEM((per, size, width), F32),
        pltpu.VMEM((rounds, slots, edge, width), BF16),
        pltpu.VMEM((rounds, slots, edge, width), BF16),
        pltpu.VMEM((3 * per + 1, edge, width), F32),
        pltpu.VMEM((3 * per + 1, edge, width), F32),
        pltpu.VMEM((3 * per + 1, edge, width), F32),
        pltpu.VMEM((per, SLOT, size), BF16),
        pltpu.VMEM((slots, SLOT, size), BF16),
        pltpu.VMEM((per, size, SLOT), BF16),
        pltpu.VMEM((slots, edge, SLOT), BF16),
        pltpu.VMEM((meta_rows, 128), jnp.int32),
        pltpu.VMEM((ns, meta_rows, 128), jnp.int32),
        pltpu.VMEM((nr, meta_rows, 128), jnp.int32),
        pltpu.VMEM((ns, nr * tr, tc), F32),
        pltpu.VMEM((ns * rows, nr * rows), BF16),
        pltpu.VMEM((ITERS, rows, width), BF16),
        pltpu.VMEM((ITERS, nr, rows, width), BF16),
        pltpu.VMEM((ITERS, ns, rows, width), BF16),
        pltpu.VMEM((ITERS, ns, rows, width), BF16),
        pltpu.VMEM((ITERS, per, SLOT, width), BF16),
        pltpu.VMEM((ITERS, slots, SLOT, width), BF16),
        dma((4 * per,)),
        dma((rounds, slots)), dma((rounds, slots)),
        dma((ns,)), dma((ns,)),
        dma((nr,)), dma((nr,)),
        dma((ns,)), dma((ns,)),
        dma((nr,)), dma((nr,)),
        dma((ITERS, nr)), dma((ITERS, nr)),
        dma((ITERS, ns)), dma((ITERS, ns)),
        dma((slots,)), dma((slots,)),
        dma((ITERS, slots)), dma((ITERS, slots)),
    ]
    out = jax.ShapeDtypeStruct(adjoint_loads.shape, F32)
    args = args[:5] + (jnp.transpose(coupling, (0, 2, 1, 3)),) + args[6:]
    results = pl.pallas_call(
        functools.partial(kernel, nr, ns),
        out_shape=(out, out),
        in_specs=[vmem, hbm, hbm, hbm, hbm, vmem, vmem, smem, smem, smem],
        out_specs=(vmem, vmem),
        scratch_shapes=scratch,
        compiler_params=pltpu.CompilerParams(
            collective_id=0, has_side_effects=True, vmem_limit_bytes=60 * 1024 * 1024
        ),
    )(*args)
    return pl.pallas_call(
        hand_over, out_shape=(out, out), in_specs=[vmem, vmem], out_specs=(vmem, vmem)
    )(*results)


def solution(mesh):
    placed = (
        P("sx", "sy", None, None, None),
        P("sx", "sy", None, None),
        P("sx", "sy", None, None),
        P("sx", "sy", None, None),
        P("sx", "sy", None, None),
        P("sx", "sy", None, None),
        P("sx", "sy"),
        P("sx", "sy"),
        P("sx", "sy", None),
        P("sx", "sy", None),
    )
    return jax.shard_map(
        functools.partial(local, mesh.shape["sx"], mesh.shape["sy"]),
        mesh=mesh,
        in_specs=placed,
        out_specs=(P("sx", "sy", None, None, None), P("sx", "sy", None, None, None)),
        check_vma=False,
    )
```
